32 devices in a mesh: dp: 16 (over z, y, x), tensor: 2 (over core).
Axes of the slice: x: 2, y: 2, z: 4, core: 2. Of those that a mesh axis runs over, the one named last changes fastest.
Arguments:
- layer_input: bfloat16 [16, 1024, 1024], P('dp', 'tensor'), may hold values from -6 to 6
- memory: bfloat16 [16, 512, 1024], P('dp', 'tensor'), may hold values from -6 to 6
- evicted: bfloat16 [16, 1536, 1024], P('dp', 'tensor'), may hold values from -6 to 6
- picture_start: int32 [16], P('dp'), may hold values from 0 to 768, as said below
- memory_lengths: int32 [16, 2], P('dp'), may hold values from 128 to 512, as said below
- w_query: bfloat16 [1024, 1024], P('dp', 'tensor'), may hold values from -0.1875 to 0.1875
- w_key: bfloat16 [1024, 1024], P('dp', 'tensor'), may hold values from -0.1875 to 0.1875
- w_value: bfloat16 [1024, 1024], P('dp', 'tensor'), may hold values from -0.1875 to 0.1875
- w_output: bfloat16 [1024, 1024], P('tensor', 'dp'), may hold values from -1.5 to 1.5
- w_compress: bfloat16 [3072, 1024], P(('dp', 'tensor')), may hold values from -0.109375 to 0.109375
- gain_attn: bfloat16 [1024], P(('dp', 'tensor')), may hold values from 0.5 to 1.5
- gain_ffn: bfloat16 [1024], P(('dp', 'tensor')), may hold values from 0.5 to 1.5
- w_inner: bfloat16 [1024, 4096], P('dp', 'tensor'), may hold values from -0.1875 to 0.1875
- w_outer: bfloat16 [4096, 1024], P('tensor', 'dp'), may hold values from -0.09375 to 0.09375
- cotangent: bfloat16 [16, 1024, 1024], P('dp', 'tensor'), may hold values from -6 to 6
Outputs:
- layer_output: bfloat16 [16, 1024, 1024], P('dp', 'tensor')
- input_grad: bfloat16 [16, 1024, 1024], P('dp', 'tensor')
- grad_query: float32 [1024, 1024], P('dp', 'tensor')
- grad_key: float32 [1024, 1024], P('dp', 'tensor')
- grad_value: float32 [1024, 1024], P('dp', 'tensor')
- grad_output_proj: float32 [1024, 1024], P('tensor', 'dp')
- grad_compress: float32 [3072, 1024], P(('dp', 'tensor'))
- grad_gain_attn: float32 [1024], P(('dp', 'tensor'))
- grad_gain_ffn: float32 [1024], P(('dp', 'tensor'))
- grad_inner: float32 [1024, 4096], P('dp', 'tensor')
- grad_outer: float32 [4096, 1024], P('tensor', 'dp')
- branch_rms: float32 [16, 3], P('dp')
The draws below stay inside these ranges and needn't reach their ends.
Inputs may be any that keep to these rules, and one draw needn't show every extreme that they name: Sequence s treats tokens picture_start[s] to picture_start[s] + 255 as one picture span; starts are multiples of half of 256. `memory_lengths`: column 0 counts the valid most recent rows of memory, column 1 those of compressed memory.
All inputs are finite; a program needn't handle non-finite values.
Results may differ from the reference program's by a relative error of at most 0.018.
Values may be sent and summed in bfloat16 or wider, within the bound.
No kernel may reach another device: no remote copies, remote signals or barrier semaphores. Data moves between devices by JAX's collectives and lax.ppermute only.
A program may use at most 256 MiB of HBM per device.

```python
import jax
import jax.numpy as jnp
from jax import lax

D = 1024
H = 8
DH = 128
FF = 4096
MEM = 512
CMEM = 512
PIC = 256
L = 1024
SEQS = 16


def draw_picture_start(key, part):
    span_steps = (L - PIC) // (PIC // 2)
    starts = jax.random.randint(key, (SEQS,), 0, span_steps + 1) * (PIC // 2)
    last_one = jnp.arange(SEQS) == SEQS - 1
    return jnp.where(last_one, L - PIC, starts).astype(jnp.int32)


def draw_memory_lengths(key, part):
    lengths = jax.random.randint(key, (SEQS, 2), MEM // 4, MEM + 1)
    first_one = jnp.arange(SEQS) == 0
    return jnp.where(first_one[:, None], MEM, lengths).astype(jnp.int32)


def steps_of(key, extent, cuts, low, high):
    gain = 1.0
    for dim, shards_of in cuts:
        draws = jax.random.uniform(jax.random.fold_in(jax.random.fold_in(key, 6), dim), (shards_of,), jnp.float32, low / len(cuts), high / len(cuts))
        gain = gain * jnp.repeat(jnp.exp(draws), extent[dim] // shards_of).reshape((-1,) + (1,) * (len(extent) - 1 - dim))
    return gain


def noise(own_key, shape, scale, most, pieces=(), held_as=jnp.bfloat16):
    level = steps_of(own_key, shape, pieces, -0.22, 0.18) if pieces else 1.0
    drawn = jax.random.normal(own_key, shape, jnp.float32) * scale * level
    return jnp.minimum(jnp.maximum(drawn, -most), most).astype(held_as)


def setup_inputs(seed: int = 0) -> dict:
    keys = jax.random.split(jax.random.key(seed), 16)
    return {
        "layer_input": noise(keys[0], (SEQS, L, D), 1.0, 6.0, ((0, 16), (1, 2))),
        "memory": noise(keys[1], (SEQS, MEM, D), 1.0, 6.0, ((0, 16), (1, 2))),
        "evicted": noise(keys[2], (SEQS, 3 * CMEM, D), 1.0, 6.0, ((0, 16), (1, 2))),
        "picture_start": draw_picture_start(jax.random.fold_in(keys[15], 71), 0),
        "memory_lengths": draw_memory_lengths(jax.random.fold_in(keys[15], 71), 0),
        "w_query": noise(keys[5], (D, H * DH), D ** -0.5, 0.1875, ((0, 16), (1, 2))),
        "w_key": noise(keys[6], (D, H * DH), D ** -0.5, 0.1875, ((0, 16), (1, 2))),
        "w_value": noise(keys[7], (D, H * DH), D ** -0.5, 0.1875, ((0, 16), (1, 2))),
        "w_output": noise(keys[8], (H * DH, D), (max(H * DH // 64, 1)) ** -0.5, 1.5, ((0, 2), (1, 16))),
        "w_compress": noise(keys[9], (3 * D, D), (3 * D) ** -0.5, 0.109375, ((0, 32),)),
        "gain_attn": jnp.clip(1.0 + 0.1 * jax.random.normal(keys[10], (D,), jnp.float32), 0.5, 1.5).astype(jnp.bfloat16),
        "gain_ffn": jnp.clip(1.0 + 0.1 * jax.random.normal(keys[11], (D,), jnp.float32), 0.5, 1.5).astype(jnp.bfloat16),
        "w_inner": noise(keys[12], (D, FF), D ** -0.5, 0.1875, ((0, 16), (1, 2))),
        "w_outer": noise(keys[13], (FF, D), FF ** -0.5, 0.09375, ((0, 2), (1, 16))),
        "cotangent": noise(keys[14], (SEQS, L, D), 1.0, 6.0, ((0, 16), (1, 2))),
    }


epsilon = 1e-06
very_negative = -1e+30

@jax.custom_vjp
def low(v):
    return lax.optimization_barrier(v.astype(jnp.bfloat16)).astype(jnp.float32)

@jax.custom_vjp
def low_back(v):
    return v

def low_keep(v):
    return (low(v), None)

def low_pass(kept, grad):
    return (grad,)

def back_keep(v):
    return (v, None)

def back_low(kept, grad):
    return (low(grad),)
low.defvjp(low_keep, low_pass)
low_back.defvjp(back_keep, back_low)

def rounded_both(value):
    return low(low_back(value))

def rms_norm(matrix_rows, gain_vec):
    return matrix_rows * lax.rsqrt(lax.optimization_barrier(jnp.mean(matrix_rows * matrix_rows, axis=-1, keepdims=True)) + epsilon) * gain_vec

def precise_dot(left_mat, right_mat):
    return jnp.dot(left_mat, right_mat, precision=lax.Precision.HIGHEST)

def allowed_keys(span_start, valid_lens):
    query_pos = jnp.arange(L, dtype=jnp.int32)[:, None]
    key_pos = jnp.arange(CMEM + MEM + L, dtype=jnp.int32)[None, :]
    comp_ok = (key_pos < CMEM) & (key_pos >= CMEM - valid_lens[1])
    mem_pos = key_pos - CMEM
    mem_ok = (mem_pos >= 0) & (mem_pos < MEM) & (mem_pos >= MEM - valid_lens[0])
    tok_pos = key_pos - CMEM - MEM
    query_pic = (query_pos >= span_start) & (query_pos < span_start + PIC)
    key_pic = (tok_pos >= span_start) & (tok_pos < span_start + PIC)
    tok_ok = (tok_pos >= 0) & ((tok_pos <= query_pos) | query_pic & key_pic)
    return comp_ok | mem_ok | tok_ok

def forward_layer(weights_all, token_rows, memory_rows, evicted_rows, allowed):
    query_weight, key_w, value_w, output_weight, compress_w, gain_a, gain_f, inner_weight, outer_weight = weights_all
    compressed = low_back(precise_dot(evicted_rows.reshape(CMEM, 3 * D), compress_w))
    keyed_rows = jnp.concatenate([compressed, memory_rows, token_rows], axis=0)
    attn_normed = low(rms_norm(keyed_rows, gain_a))
    query_rows = rounded_both(precise_dot(attn_normed[CMEM + MEM:], query_weight)).reshape(L, H, DH)
    key_rows = rounded_both(precise_dot(attn_normed, key_w)).reshape(CMEM + MEM + L, H, DH)
    value_rows = rounded_both(precise_dot(attn_normed, value_w)).reshape(CMEM + MEM + L, H, DH)
    scores = low_back(DH ** (-0.5) * jnp.einsum('qhd,khd->hqk', query_rows, key_rows, precision=lax.Precision.HIGHEST))
    scores = jnp.where(allowed[None], scores, very_negative)
    attn_probs = jax.nn.softmax(scores, axis=-1)
    mixed_heads = rounded_both(jnp.einsum('hqk,khd->qhd', low(attn_probs), value_rows, precision=lax.Precision.HIGHEST).reshape(L, H * DH))
    attn_branch = low_back(precise_dot(mixed_heads, output_weight))
    after_attn = token_rows + attn_branch
    ffn_normed = low(rms_norm(after_attn, gain_f))
    inner_hidden = low_back(precise_dot(ffn_normed, inner_weight))
    hidden_active = low(jax.nn.gelu(inner_hidden, approximate=True))
    ffn_branch = low_back(precise_dot(hidden_active, outer_weight))
    return (after_attn + ffn_branch, (attn_branch, ffn_branch))

def reference(layer_input, memory, evicted, picture_start, memory_lengths, w_query, w_key, w_value, w_output, w_compress, gain_attn, gain_ffn, w_inner, w_outer, cotangent):
    weights_all = tuple((weight.astype(jnp.float32) for weight in (w_query, w_key, w_value, w_output, w_compress, gain_attn, gain_ffn, w_inner, w_outer)))

    def per_sequence(grad_sums, seq_items):
        token_rows, memory_rows, evicted_rows, span_start, valid_lens, incoming_row_grads = seq_items
        allowed = allowed_keys(span_start, valid_lens)
        memory_f = memory_rows.astype(jnp.float32)
        evicted_f = evicted_rows.astype(jnp.float32)

        def forward_fn(weights_in, tokens_in):
            return forward_layer(weights_in, tokens_in, memory_f, evicted_f, allowed)
        summed, pull_back, branches = jax.vjp(forward_fn, weights_all, token_rows.astype(jnp.float32), has_aux=True)
        weight_grads, token_grad = pull_back(incoming_row_grads.astype(jnp.float32))
        attn_branch, ffn_branch = branches
        sizes_rms = jnp.stack([jnp.sqrt(jnp.mean(attn_branch * attn_branch)), jnp.sqrt(jnp.mean(ffn_branch * ffn_branch)), jnp.sqrt(jnp.mean(summed * summed))])
        new_sums = jax.tree.map(jnp.add, grad_sums, weight_grads)
        return (new_sums, (summed.astype(jnp.bfloat16), token_grad.astype(jnp.bfloat16), sizes_rms))
    zeros_all = jax.tree.map(jnp.zeros_like, weights_all)
    grad_sums, outputs_all = lax.scan(per_sequence, zeros_all, (layer_input, memory, evicted, picture_start, memory_lengths, cotangent))
    layer_output, input_grad, branch_rms = outputs_all
    return (layer_output, input_grad, grad_sums[0], grad_sums[1], grad_sums[2], grad_sums[3], grad_sums[4], grad_sums[5], grad_sums[6], grad_sums[7], grad_sums[8], branch_rms)
```

```python
import jax
import jax.numpy as jnp
from jax import lax
from jax.experimental import pallas as pl
from jax.experimental.pallas import tpu as pltpu
from jax.sharding import PartitionSpec as P


D = 1024
DH = 128
MEM = 512
CMEM = 512
PIC = 256
L = 1024

epsilon = 1e-06
very_negative = -1e30
F32 = jnp.float32
BF16 = jnp.bfloat16
AXES = ("dp", "tensor")


def matmul(a, b, dims, out=F32):
    return lax.dot_general(a, b, (dims, ((), ())), preferred_element_type=F32).astype(out)


def nn(a, b, out=F32):
    return matmul(a, b, ((1,), (0,)), out)


def nt(a, b, out=F32):
    return matmul(a, b, ((1,), (1,)), out)


def tn(a, b, out=F32):
    return matmul(a, b, ((0,), (0,)), out)


class Cube:
    def __init__(self, n, cores):
        self.n, self.cores = n, cores
        self.steps = n.bit_length() - 1
        low = list(range(min(2, self.steps)))
        high = list(range(2, self.steps))
        self.order = [high + (low[::-1] if c % 2 == 0 else low) for c in range(cores)]
        self.masks = [
            [sum(1 << o[s] for s in range(self.steps) if (j >> s) & 1) for j in range(n)]
            for o in self.order
        ]
        self.dp = lax.axis_index("dp")
        self.core = lax.axis_index("tensor")
        table = jnp.array(self.masks, jnp.int32)
        self.own = lax.dynamic_index_in_dim(table, self.core, 0, keepdims=False) ^ self.dp
        self.sibling = (
            lax.dynamic_index_in_dim(table, self.cores - 1 - self.core, 0, keepdims=False) ^ self.dp
        )

    def swap(self, value, step):
        pairs = [
            (d * self.cores + c, (d ^ (1 << self.order[c][step])) * self.cores + c)
            for d in range(self.n)
            for c in range(self.cores)
        ]
        return lax.ppermute(value, AXES, pairs)

    def core_swap(self, value):
        return lax.ppermute(value, "tensor", [(0, 1), (1, 0)])

    def gather(self, shard):
        held = shard[None]
        for step in range(self.steps - 1):
            held = jnp.concatenate([held, self.swap(held, step)], axis=0)
        return held, self.swap(held, self.steps - 1)

    def reduce(self, blocks):
        for step in reversed(range(self.steps)):
            half = blocks.shape[0] // 2
            arrived = self.swap(blocks[half:], step)
            total = blocks[:half].astype(F32) + arrived.astype(F32)
            blocks = total.astype(BF16) if step else total
        return blocks[0]


def place(first, second, where, total):
    count, rows, cols = first.shape

    def body(where_ref, a_ref, b_ref, o_ref):
        j = pl.program_id(0)

        @pl.when(j < count)
        def _():
            o_ref[...] = a_ref[...]

        @pl.when(j >= count)
        def _():
            o_ref[...] = b_ref[...]

    return pl.pallas_call(
        body,
        out_shape=jax.ShapeDtypeStruct((total, rows, cols), first.dtype),
        grid_spec=pltpu.PrefetchScalarGridSpec(
            num_scalar_prefetch=1,
            grid=(2 * count,),
            in_specs=[
                pl.BlockSpec((1, rows, cols), lambda j, w: (jnp.minimum(j, count - 1), 0, 0)),
                pl.BlockSpec((1, rows, cols), lambda j, w: (jnp.maximum(j - count, 0), 0, 0)),
            ],
            out_specs=pl.BlockSpec((1, rows, cols), lambda j, w: (w[j], 0, 0)),
        ),
        name="place",
    )(where, first, second)


def pick(blocks, where):
    _, rows, cols = blocks.shape
    count = where.shape[0]

    def body(where_ref, a_ref, o_ref):
        o_ref[...] = a_ref[...]

    return pl.pallas_call(
        body,
        out_shape=jax.ShapeDtypeStruct((count, rows, cols), blocks.dtype),
        grid_spec=pltpu.PrefetchScalarGridSpec(
            num_scalar_prefetch=1,
            grid=(count,),
            in_specs=[pl.BlockSpec((1, rows, cols), lambda j, w: (w[j], 0, 0))],
            out_specs=pl.BlockSpec((1, rows, cols), lambda j, w: (j, 0, 0)),
        ),
        name="pick",
    )(where, blocks)


def rms_norm(matrix_rows, gain_vec):
    return (
        matrix_rows
        * lax.rsqrt(jnp.mean(matrix_rows * matrix_rows, axis=-1, keepdims=True) + epsilon)
        * gain_vec
    )


def gelu_tanh(inner_in):
    return jax.nn.gelu(inner_in, approximate=True)


def allowed_keys(core, span_start, valid_lens, comp_part, mem_part, tok_part):
    halves = (core, 1 - core)
    query_pos = jnp.concatenate([h * tok_part + jnp.arange(tok_part) for h in halves])[:, None]
    columns = []
    for h in halves:
        comp = h * comp_part + jnp.arange(comp_part)[None, :]
        mem = h * mem_part + jnp.arange(mem_part)[None, :]
        tok = h * tok_part + jnp.arange(tok_part)[None, :]
        ones = jnp.ones_like(query_pos) > 0
        columns.append((comp >= CMEM - valid_lens[1]) & ones)
        columns.append((mem >= MEM - valid_lens[0]) & ones)
        query_pic = (query_pos >= span_start) & (query_pos < span_start + PIC)
        key_pic = (tok >= span_start) & (tok < span_start + PIC)
        columns.append((tok <= query_pos) | query_pic & key_pic)
    return jnp.concatenate(columns, axis=1)


def masked_scores(query_rows, key_rows, allowed):
    scores = DH ** (-0.5) * jnp.einsum(
        "qhd,khd->hqk", query_rows, key_rows, preferred_element_type=F32
    )
    return jnp.where(allowed[None], scores, very_negative)


def attend(query_rows, key_rows, value_rows, allowed):
    scores = masked_scores(query_rows, key_rows, allowed)
    row_max = jnp.max(scores, axis=-1, keepdims=True)
    shifted = jnp.exp(scores - row_max)
    row_total = jnp.sum(shifted, axis=-1, keepdims=True)
    attn_probs = (shifted / row_total).astype(BF16)
    mixed = jnp.einsum("hqk,khd->qhd", attn_probs, value_rows, preferred_element_type=F32)
    return mixed.astype(BF16), row_max + jnp.log(row_total)


def attend_back(query_rows, key_rows, value_rows, d_mixed, log_total, allowed):
    scores = masked_scores(query_rows, key_rows, allowed)
    attn_probs = jnp.exp(scores - log_total)
    d_probs = jnp.einsum("qhd,khd->hqk", d_mixed, value_rows, preferred_element_type=F32)
    d_values = jnp.einsum(
        "hqk,qhd->khd", attn_probs.astype(BF16), d_mixed, preferred_element_type=F32
    )
    d_scores = (
        attn_probs * (d_probs - jnp.sum(attn_probs * d_probs, axis=-1, keepdims=True))
    ).astype(BF16)
    d_queries = DH ** (-0.5) * jnp.einsum(
        "hqk,khd->qhd", d_scores, key_rows, preferred_element_type=F32
    )
    d_keys = DH ** (-0.5) * jnp.einsum(
        "hqk,qhd->khd", d_scores, query_rows, preferred_element_type=F32
    )
    return d_queries.astype(BF16), d_keys.astype(BF16), d_values.astype(BF16)


def per_device(
    layer_input,
    memory,
    evicted,
    picture_start,
    memory_lengths,
    w_query,
    w_key,
    w_value,
    w_output,
    w_compress,
    gain_attn,
    gain_ffn,
    w_inner,
    w_outer,
    cotangent,
):
    cube = Cube(lax.axis_size("dp"), lax.axis_size("tensor"))
    n, core = cube.n, cube.core
    tokens, memory, evicted, cotangent = layer_input[0], memory[0], evicted[0], cotangent[0]
    tok_part, mem_part, comp_part = tokens.shape[0], memory.shape[0], evicted.shape[0] // 3
    width = w_query.shape[1]
    heads = width // DH
    rows = comp_part + mem_part + tok_part

    def both(own, other, axis=-1):
        flip = core > 0
        return jnp.concatenate(
            [jnp.where(flip, other, own), jnp.where(flip, own, other)], axis=axis
        )

    gains_own = jnp.concatenate([gain_attn[None], gain_ffn[None]], axis=0)
    gain_shard = both(gains_own, cube.core_swap(gains_own))
    gain_a, gain_b = cube.gather(gain_shard)
    order = jnp.argsort(cube.own)
    gains = jnp.concatenate([gain_a, gain_b], axis=0)[order]
    gains = jnp.transpose(gains, (1, 0, 2)).reshape(2, D).astype(F32)
    gain_attn_f, gain_ffn_f = gains[0], gains[1]

    def gathered(shard):
        first, second = cube.gather(shard)
        return place(first, second, cube.own, n).reshape(-1, shard.shape[1])

    qkv_w = gathered(jnp.concatenate([w_query, w_key, w_value], axis=1))
    compress_a, compress_b = cube.gather(w_compress)
    compress_own = jnp.concatenate([compress_a, compress_b], axis=0)
    compress_sib = cube.core_swap(compress_own)
    compress_where = jnp.concatenate(
        [cube.own * 2 + core, cube.sibling * 2 + (1 - core)], axis=0
    )
    compress_w = place(compress_own, compress_sib, compress_where, 2 * n).reshape(-1, D)
    out_inner_w = gathered(jnp.concatenate([w_output.T, w_inner], axis=1))
    outer_t = gathered(w_outer.T)
    query_w, key_w, value_w = (qkv_w[:, i * width : (i + 1) * width] for i in range(3))
    output_t, inner_w = out_inner_w[:, :width], out_inner_w[:, width:]

    grouped = evicted.reshape(comp_part, 3 * D)
    compressed = nn(grouped, compress_w)
    token_f = tokens.astype(F32)
    keyed_rows = jnp.concatenate([compressed, memory.astype(F32), token_f], axis=0)
    attn_value, attn_pull = jax.vjp(rms_norm, keyed_rows, gain_attn_f)
    attn_normed = attn_value.astype(BF16)
    all_rows = jnp.concatenate([attn_normed, cube.core_swap(attn_normed)], axis=0)
    tok_at = comp_part + mem_part
    token_rows = jnp.concatenate([all_rows[tok_at:rows], all_rows[rows + tok_at :]], axis=0)
    query_rows = nn(token_rows, query_w, BF16).reshape(-1, heads, DH)
    key_rows = nn(all_rows, key_w, BF16).reshape(-1, heads, DH)
    value_rows = nn(all_rows, value_w, BF16).reshape(-1, heads, DH)
    allowed = allowed_keys(
        core, picture_start[0], memory_lengths[0], comp_part, mem_part, tok_part
    )
    mixed, log_total = attend(query_rows, key_rows, value_rows, allowed)
    mixed = mixed.reshape(-1, width)
    branch = nt(mixed, output_t)
    attn_branch = branch[:tok_part] + cube.core_swap(branch[tok_part:].astype(BF16)).astype(F32)
    after_attn = token_f + attn_branch
    ffn_value, ffn_pull = jax.vjp(rms_norm, after_attn, gain_ffn_f)
    ffn_own = ffn_value.astype(BF16)
    ffn_rows = jnp.concatenate([ffn_own, cube.core_swap(ffn_own)], axis=0)
    inner_hidden = nn(ffn_rows, inner_w)
    active_f, gelu_pull = jax.vjp(gelu_tanh, inner_hidden)
    active = active_f.astype(BF16)
    ffn_share = nt(active, outer_t)
    ffn_branch = ffn_share[:tok_part] + cube.core_swap(ffn_share[tok_part:].astype(BF16)).astype(
        F32
    )
    summed = after_attn + ffn_branch
    layer_output = summed.astype(BF16)
    square_sums = jnp.stack(
        [
            jnp.sum(attn_branch * attn_branch),
            jnp.sum(ffn_branch * ffn_branch),
            jnp.sum(summed * summed),
        ]
    )
    branch_rms = jnp.sqrt((square_sums + cube.core_swap(square_sums)) / (L * D))[None]

    def reduced(partial, block_rows):
        blocks = partial.reshape(n, block_rows, -1)
        return cube.reduce(pick(blocks, cube.own))

    out_grads = jnp.concatenate([cotangent, cube.core_swap(cotangent)], axis=0)
    grad_outer = reduced(tn(out_grads, active, BF16), D // n).T
    d_active = nn(out_grads, outer_t)
    d_inner = gelu_pull(d_active)[0].astype(BF16)
    d_ffn_share = nt(d_inner, inner_w)
    d_ffn_normed = d_ffn_share[:tok_part] + cube.core_swap(
        d_ffn_share[tok_part:].astype(BF16)
    ).astype(F32)
    d_after, d_gain_ffn = ffn_pull(d_ffn_normed)
    grad_after = cotangent.astype(F32) + d_after
    grad_after_own = grad_after.astype(BF16)
    attn_grads = jnp.concatenate([grad_after_own, cube.core_swap(grad_after_own)], axis=0)
    out_inner = reduced(
        jnp.concatenate([tn(attn_grads, mixed, BF16), tn(ffn_rows, d_inner, BF16)], axis=1), D // n
    )
    grad_output, grad_inner = out_inner[:, :width].T, out_inner[:, width:]
    d_mixed = nn(attn_grads, output_t, BF16)
    d_queries, d_keys, d_values = attend_back(
        query_rows,
        key_rows,
        value_rows,
        d_mixed.reshape(-1, heads, DH),
        log_total,
        allowed,
    )
    d_queries, d_keys, d_values = (v.reshape(-1, width) for v in (d_queries, d_keys, d_values))
    qkv = reduced(
        jnp.concatenate(
            [
                tn(token_rows, d_queries, BF16),
                tn(all_rows, d_keys, BF16),
                tn(all_rows, d_values, BF16),
            ],
            axis=1,
        ),
        D // n,
    )
    grad_query, grad_key, grad_value = (qkv[:, i * width : (i + 1) * width] for i in range(3))
    d_rows = nt(d_keys, key_w) + nt(d_values, value_w)
    d_tok = nt(d_queries, query_w)
    d_own = jnp.concatenate([d_rows[:tok_at], d_rows[tok_at:rows] + d_tok[:tok_part]], axis=0)
    d_other = jnp.concatenate(
        [d_rows[rows : rows + tok_at], d_rows[rows + tok_at :] + d_tok[tok_part:]], axis=0
    ).astype(BF16)
    d_attn_normed = d_own + cube.core_swap(d_other).astype(F32)
    d_keyed, d_gain_attn = attn_pull(d_attn_normed)
    input_grad = (grad_after + d_keyed[tok_at:]).astype(BF16)
    d_compressed = d_keyed[:comp_part].astype(BF16)
    compress_part = tn(grouped, d_compressed, BF16).reshape(2 * n, -1, D)
    own_part = pick(compress_part, cube.own * 2 + core)
    sib_part = pick(compress_part, cube.sibling * 2 + (1 - core))
    own_sum = (own_part.astype(F32) + cube.core_swap(sib_part).astype(F32)).astype(BF16)
    grad_compress = cube.reduce(own_sum)
    d_gains = jnp.stack([d_gain_attn, d_gain_ffn])
    d_gains = d_gains + cube.core_swap(d_gains)
    share = gain_attn.shape[0]
    d_gains = d_gains.reshape(2, n, cube.cores, share)
    d_gains = lax.dynamic_index_in_dim(d_gains, core, 2, keepdims=False)
    d_gains = jnp.transpose(d_gains, (1, 0, 2))[cube.own]
    for step in reversed(range(cube.steps)):
        half = d_gains.shape[0] // 2
        d_gains = d_gains[:half] + cube.swap(d_gains[half:], step)
    return (
        layer_output[None],
        input_grad[None],
        grad_query,
        grad_key,
        grad_value,
        grad_output,
        grad_compress,
        d_gains[0, 0],
        d_gains[0, 1],
        grad_inner,
        grad_outer,
        branch_rms,
    )


def solution(mesh):
    in_specs = (
        P("dp", "tensor", None),
        P("dp", "tensor", None),
        P("dp", "tensor", None),
        P("dp"),
        P("dp", None),
        P("dp", "tensor"),
        P("dp", "tensor"),
        P("dp", "tensor"),
        P("tensor", "dp"),
        P(("dp", "tensor"), None),
        P(("dp", "tensor")),
        P(("dp", "tensor")),
        P("dp", "tensor"),
        P("tensor", "dp"),
        P("dp", "tensor", None),
    )
    out_specs = (
        P("dp", "tensor", None),
        P("dp", "tensor", None),
        P("dp", "tensor"),
        P("dp", "tensor"),
        P("dp", "tensor"),
        P("tensor", "dp"),
        P(("dp", "tensor"), None),
        P(("dp", "tensor")),
        P(("dp", "tensor")),
        P("dp", "tensor"),
        P("tensor", "dp"),
        P("dp", None),
    )
    return jax.shard_map(
        per_device, mesh=mesh, in_specs=in_specs, out_specs=out_specs, check_vma=False
    )
```

```python
import jax
import jax.numpy as jnp
from jax import lax
from jax.experimental import pallas as pl
from jax.experimental.pallas import tpu as pltpu
from jax.sharding import PartitionSpec as P


D = 1024
DH = 128
MEM = 512
CMEM = 512
PIC = 256
L = 1024

epsilon = 1e-06
very_negative = -1e30


F32 = jnp.float32
BF16 = jnp.bfloat16
AXES = ("dp", "tensor")


def matmul(a, b, dims, out=F32):
    return lax.dot_general(a, b, (dims, ((), ())), preferred_element_type=F32).astype(out)


def nn(a, b, out=F32):
    return matmul(a, b, ((1,), (0,)), out)


def nt(a, b, out=F32):
    return matmul(a, b, ((1,), (1,)), out)


def tn(a, b, out=F32):
    return matmul(a, b, ((0,), (0,)), out)


class Cube:
    def __init__(self, n, cores):
        self.n, self.cores = n, cores
        self.far = n // 4
        self.low = [(1, 0) if c % 2 == 0 else (0, 1) for c in range(cores)]
        self.masks = [
            [
                (j % self.far) * 4
                + ((j // self.far) & 1) * (1 << first)
                + (j // (2 * self.far)) * (1 << second)
                for j in range(n)
            ]
            for first, second in self.low
        ]
        self.dp = lax.axis_index("dp")
        self.core = lax.axis_index("tensor")
        table = jnp.array(self.masks, jnp.int32)
        self.own = lax.dynamic_index_in_dim(table, self.core, 0, keepdims=False) ^ self.dp

    def send(self, value, flips):
        pairs = [
            (d * self.cores + c, (d ^ flips[c]) * self.cores + c)
            for d in range(self.n)
            for c in range(self.cores)
        ]
        return lax.ppermute(value, AXES, pairs)

    def far_send(self, value, m):
        return self.send(value, [4 * m] * self.cores)

    def low_swap(self, value, which):
        return self.send(value, [1 << pair[which] for pair in self.low])

    def core_swap(self, value):
        return lax.ppermute(value, "tensor", [(0, 1), (1, 0)])

    def reduce(self, low, high):
        arrived = self.low_swap(high, 1)
        half = low.shape[0] // 2

        def added(part, other, run):
            return part[run].astype(F32) + other[run].astype(F32)

        far = slice(half, None)
        near = added(low, arrived, slice(0, half))
        far_sum = added(low, arrived, far).astype(BF16)
        arrived = self.low_swap(far_sum, 0)
        total = near[0] + arrived[0].astype(F32)
        sent = [
            self.far_send(added(near, arrived, slice(m, m + 1)).astype(BF16), m)
            for m in range(1, self.far)
        ]
        for block in sent:
            total = total + block[0].astype(F32)
        return total


ANY = pl.BlockSpec(memory_space=pl.ANY)
SMEM = pl.BlockSpec(memory_space=pltpu.SMEM)
VMEM = pl.BlockSpec(memory_space=pltpu.VMEM)


def run_copies(copies):
    for copy in copies:
        copy.start()
    for copy in copies:
        copy.wait()


def place(parts, where, pieces, outs):
    rows = parts[0].shape[1]
    count = where.shape[0]

    def body(where_ref, *refs):
        ins, out_refs, sem = refs[: len(parts)], refs[len(parts) : -1], refs[-1]
        copies, j = [], 0
        for source in ins:
            for b in range(source.shape[0]):
                at = 0
                for i, (width, out, row) in enumerate(pieces):
                    copies.append(
                        pltpu.make_async_copy(
                            source.at[b, :, pl.ds(at, width)],
                            out_refs[out].at[where_ref[j], pl.ds(row, rows)],
                            sem.at[j * len(pieces) + i],
                        )
                    )
                    at += width
                j += 1
        run_copies(copies)

    filled = pl.pallas_call(
        body,
        out_shape=[jax.ShapeDtypeStruct((count, r, w), parts[0].dtype) for r, w in outs],
        in_specs=[SMEM] + [ANY] * len(parts),
        out_specs=[VMEM] * len(outs),
        scratch_shapes=[pltpu.SemaphoreType.DMA((count * len(pieces),))],
        name="place",
    )(where, *parts)
    return [o.reshape(count * r, w) for o, (r, w) in zip(filled, outs)]


def pick(blocks, where, below=None):
    count = where.shape[0]
    rows = blocks[0].shape[1]
    width = sum(b.shape[2] for b in blocks)
    half = count // 2
    ins = list(blocks) + ([] if below is None else [below])
    total = rows + (0 if below is None else below.shape[1])

    def body(where_ref, *refs):
        sources, (low, high, sem) = refs[: len(ins)], refs[len(ins) :]
        copies = []
        for j in range(count):
            at = 0
            out = (low if j < half else high).at[j % half]
            for i, source in enumerate(sources):
                if i < len(blocks):
                    target = out.at[pl.ds(0, rows), pl.ds(at, source.shape[2])]
                    at += source.shape[2]
                else:
                    target = out.at[pl.ds(rows, source.shape[1])]
                copies.append(
                    pltpu.make_async_copy(
                        source.at[where_ref[j]], target, sem.at[j * len(ins) + i]
                    )
                )
        run_copies(copies)

    return pl.pallas_call(
        body,
        out_shape=[jax.ShapeDtypeStruct((half, total, width), BF16)] * 2,
        in_specs=[SMEM] + [ANY] * len(ins),
        out_specs=[VMEM] * 2,
        scratch_shapes=[pltpu.SemaphoreType.DMA((count * len(ins),))],
        name="pick",
    )(where, *ins)


def rms_norm(matrix_rows, gain_vec):
    return (
        matrix_rows
        * lax.rsqrt(jnp.mean(matrix_rows * matrix_rows, axis=-1, keepdims=True) + epsilon)
        * gain_vec
    )


def gelu_tanh(inner_in):
    return jax.nn.gelu(inner_in, approximate=True)


LOG2E = 1.4426950408889634


def key_runs(core, half, kind, part_rows, comp_part, mem_part):
    base = jnp.bitwise_xor(core, half) * part_rows
    offset = {"comp": 0, "mem": comp_part, "tok": comp_part + mem_part}[kind]
    return pl.multiple_of(base + offset, 128)


def attention_chunks(info, q_half, shapes):
    comp_part, mem_part, tok_part = shapes
    part_rows = comp_part + mem_part + tok_part
    core, span, mem_len, comp_len = info[0], info[1], info[2], info[3]

    def start(kind, half):
        return key_runs(core, half, kind, part_rows, comp_part, mem_part)

    def tail(first, total, length):
        def masker(shape):
            row = lax.broadcasted_iota(jnp.int32, shape, 0) + first
            return row >= total - length

        return masker

    def causal(half):
        def masker(shape):
            key = lax.broadcasted_iota(jnp.int32, shape, 0) + half * tok_part
            query = lax.broadcasted_iota(jnp.int32, shape, 1) + q_half * tok_part
            key_in = (key >= span) & (key < span + PIC)
            query_in = (query >= span) & (query < span + PIC)
            return (key <= query) | (key_in & query_in)

        return masker

    chunks = []
    for half in (0, 1):
        chunks.append((start("comp", half), comp_part, tail(half * comp_part, CMEM, comp_len), None))
    for half in (0, 1):
        chunks.append((start("mem", half), mem_part, tail(half * mem_part, MEM, mem_len), None))
    crosses = (span < tok_part) & (span + PIC > tok_part)
    chunks.append((start("tok", 0), tok_part, None, q_half == 1))
    chunks.append((start("tok", 0), tok_part, causal(0), q_half == 0))
    chunks.append((start("tok", 1), tok_part, causal(1), (q_half == 1) | crosses))
    return chunks


def attend(info, query_rows, keyval, shapes, heads):
    rows = keyval.shape[0]
    q_part = query_rows.shape[0] // 2
    factor = DH ** (-0.5) * LOG2E

    def body(info_ref, q_ref, kv_ref, o_ref, lse_ref, vt_ref, m_ref, l_ref, acc_ref):
        q_half = pl.program_id(1)

        @pl.when(q_half == 0)
        def _():
            vt_ref[...] = kv_ref[:, DH:].T

        m_ref[...] = jnp.full_like(m_ref, very_negative)
        l_ref[...] = jnp.zeros_like(l_ref)
        acc_ref[...] = jnp.zeros_like(acc_ref)
        q = q_ref[...]
        for first, count, masker, needed in attention_chunks(info_ref, q_half, shapes):

            def step(first=first, count=count, masker=masker):
                s = nt(kv_ref[pl.ds(first, count), :DH], q)
                if masker is not None:
                    s = jnp.where(masker(s.shape), s, very_negative)
                m_old = m_ref[...]
                m_new = jnp.maximum(m_old, jnp.max(s, axis=0, keepdims=True))
                shrink = jnp.exp2((m_old - m_new) * factor)
                p = jnp.exp2((s - m_new) * factor)
                l_ref[...] = l_ref[...] * shrink + jnp.sum(p, axis=0, keepdims=True)
                acc_ref[...] = acc_ref[...] * shrink + nn(
                    vt_ref[:, pl.ds(first, count)], p.astype(BF16)
                )
                m_ref[...] = m_new

            if needed is None:
                step()
            else:
                pl.when(needed)(step)
        total = l_ref[...]
        o_ref[...] = (acc_ref[...] / total).T.astype(BF16)
        lse_ref[...] = (m_ref[...] * factor + jnp.log2(total))[None]

    def q_map(h, a, info_ref):
        return (jnp.bitwise_xor(a, info_ref[0]), h)

    return pl.pallas_call(
        body,
        out_shape=(
            jax.ShapeDtypeStruct(query_rows.shape, BF16),
            jax.ShapeDtypeStruct((heads * 2, 1, q_part), F32),
        ),
        grid_spec=pltpu.PrefetchScalarGridSpec(
            num_scalar_prefetch=1,
            grid=(heads, 2),
            in_specs=[
                pl.BlockSpec((q_part, DH), q_map),
                pl.BlockSpec((rows, 2 * DH), lambda h, a, i: (0, h)),
            ],
            out_specs=[
                pl.BlockSpec((q_part, DH), q_map),
                pl.BlockSpec((1, 1, q_part), lambda h, a, i: (h * 2 + a, 0, 0)),
            ],
            scratch_shapes=[
                pltpu.VMEM((DH, rows), BF16),
                pltpu.VMEM((1, q_part), F32),
                pltpu.VMEM((1, q_part), F32),
                pltpu.VMEM((DH, q_part), F32),
            ],
        ),
        name="attend",
    )(info, query_rows, keyval)


def attend_back(info, query_rows, keyval, mixed, d_mixed, lse, shapes, skip, heads, carry=None):
    rows = keyval.shape[0]
    q_part = query_rows.shape[0] // 2
    scale = DH ** (-0.5)
    factor = scale * LOG2E

    def body(info_ref, q_ref, kv_ref, o_ref, g_ref, lse_ref, *refs):
        dq_ref, dkv_ref, kt_ref, dk_acc, dv_acc, dq_acc = refs[-6:]
        q_half = pl.program_id(1)

        @pl.when(q_half == 0)
        def _():
            kt_ref[...] = kv_ref[:, :DH].T
            dk_acc[...] = jnp.zeros_like(dk_acc)
            dv_acc[...] = jnp.zeros_like(dv_acc)

        dq_acc[...] = jnp.zeros_like(dq_acc)
        q, g = q_ref[...], g_ref[...]
        lse_row = lse_ref[0]
        delta = jnp.sum((g.astype(F32) * o_ref[...].astype(F32)).T, axis=0, keepdims=True)
        for first, count, masker, needed in attention_chunks(info_ref, q_half, shapes):

            def step(first=first, count=count, masker=masker):
                run = pl.ds(first, count)
                p = jnp.exp2(nt(kv_ref[run, :DH], q) * factor - lse_row)
                if masker is not None:
                    p = jnp.where(masker(p.shape), p, 0.0)
                d_p = nt(kv_ref[run, DH:], g)
                d_s = (p * (d_p - delta)).astype(BF16)
                dv_acc[run, :] += nn(p.astype(BF16), g)
                dk_acc[run, :] += nn(d_s, q)
                dq_acc[...] += nn(kt_ref[:, run], d_s)

            if needed is None:
                step()
            else:
                pl.when(needed)(step)
        dq_ref[...] = (dq_acc[...] * scale).T.astype(BF16)

        @pl.when(q_half == 1)
        def _():
            dkv_ref[:, :DH] = (dk_acc[...] * scale).astype(BF16)
            dkv_ref[:, DH:] = dv_acc[...].astype(BF16)

    def q_map(h, a, info_ref):
        return (jnp.bitwise_xor(a, info_ref[0]), h + skip)

    q_spec = pl.BlockSpec((q_part, DH), q_map)
    kv_spec = pl.BlockSpec((rows, 2 * DH), lambda h, a, i: (0, h + skip))
    lse_spec = pl.BlockSpec((1, 1, q_part), lambda h, a, i: ((h + skip) * 2 + a, 0, 0))
    carried = [] if carry is None else list(carry)
    return pl.pallas_call(
        body,
        out_shape=(
            jax.ShapeDtypeStruct(query_rows.shape, BF16),
            jax.ShapeDtypeStruct(keyval.shape, BF16),
        ),
        grid_spec=pltpu.PrefetchScalarGridSpec(
            num_scalar_prefetch=1,
            grid=(heads, 2),
            in_specs=[q_spec, kv_spec, q_spec, q_spec, lse_spec] + [ANY] * len(carried),
            out_specs=[q_spec, kv_spec],
            scratch_shapes=[
                pltpu.VMEM((DH, rows), BF16),
                pltpu.VMEM((rows, DH), F32),
                pltpu.VMEM((rows, DH), F32),
                pltpu.VMEM((DH, q_part), F32),
            ],
        ),
        input_output_aliases={6 + i: i for i in range(len(carried))},
        name="attend_back",
    )(info, query_rows, keyval, mixed, d_mixed, lse, *carried)


def per_device(
    layer_input,
    memory,
    evicted,
    picture_start,
    memory_lengths,
    w_query,
    w_key,
    w_value,
    w_output,
    w_compress,
    gain_attn,
    gain_ffn,
    w_inner,
    w_outer,
    cotangent,
):
    cube = Cube(lax.axis_size("dp"), lax.axis_size("tensor"))
    n, core = cube.n, cube.core
    tokens, memory, evicted, cotangent = layer_input[0], memory[0], evicted[0], cotangent[0]
    tok_part, mem_part, comp_part = tokens.shape[0], memory.shape[0], evicted.shape[0] // 3
    parts = (comp_part, mem_part, tok_part)
    width = w_query.shape[1]
    heads = width // DH
    rows = comp_part + mem_part + tok_part
    inner_width = w_inner.shape[1]
    share = gain_attn.shape[0]
    shard_rows = w_query.shape[0]

    def by_core(own, other, axis):
        flip = core > 0
        return jnp.concatenate(
            [jnp.where(flip, other, own), jnp.where(flip, own, other)], axis=axis
        )

    def gathered(shard, pieces, outs):
        held = [shard[None]] + [cube.far_send(shard[None], m) for m in range(1, cube.far)]
        held = jnp.concatenate(held, axis=0)
        arrived = cube.low_swap(held, 0)
        held = jnp.concatenate([held, arrived], axis=0)
        arrived = cube.low_swap(held, 1)
        return place([held, arrived], cube.own, pieces, outs)

    def picked(blocks, below=None):
        return pick(blocks, cube.own, below)

    col_half = D // 2
    send_cols = jnp.where(core > 0, w_compress[:, :col_half], w_compress[:, col_half:])
    keep_cols = jnp.where(core > 0, w_compress[:, col_half:], w_compress[:, :col_half])
    compress_cols = by_core(keep_cols, cube.core_swap(send_cols), 0)
    gains_own = jnp.stack([gain_attn, gain_ffn])
    gain_pair = by_core(gains_own[None], cube.core_swap(gains_own)[None], 0)
    gain_row = jnp.pad(gain_pair.reshape(1, -1), ((0, shard_rows - 1), (0, 128 - 4 * share)))
    columns = [w_query]
    for h in range(heads):
        head = slice(h * DH, (h + 1) * DH)
        columns += [w_key[:, head], w_value[:, head]]
    columns += [gain_row]
    folds = compress_cols.shape[0] // shard_rows
    columns += [compress_cols[i * shard_rows : (i + 1) * shard_rows] for i in range(folds)]
    query_w, keyval_w, gain_rows, compress_w = gathered(
        jnp.concatenate(columns, axis=1),
        [(width, 0, 0), (2 * width, 1, 0), (128, 2, 0)]
        + [(col_half, 3, i * shard_rows) for i in range(folds)],
        [
            (shard_rows, width),
            (shard_rows, 2 * width),
            (shard_rows, 128),
            (folds * shard_rows, col_half),
        ],
    )
    output_t, inner_w = gathered(
        jnp.concatenate([w_output.T, w_inner], axis=1),
        [(width, 0, 0), (inner_width, 1, 0)],
        [(shard_rows, width), (shard_rows, inner_width)],
    )
    (outer_t,) = gathered(w_outer.T, [(inner_width, 0, 0)], [(shard_rows, inner_width)])
    gains = gain_rows.reshape(n, shard_rows, 128)[:, 0, : 4 * share].reshape(n, 2, 2, share)
    gains = jnp.transpose(gains, (2, 0, 1, 3)).reshape(2, D).astype(F32)
    gain_attn_f, gain_ffn_f = gains[0], gains[1]

    info = jnp.concatenate([core[None], picture_start, memory_lengths[0]]).astype(jnp.int32)
    grouped_own = evicted.reshape(comp_part, 3 * D)
    grouped = jnp.concatenate([grouped_own, cube.core_swap(grouped_own)], axis=0)
    grouped_t = lax.optimization_barrier(grouped.T)
    comp_cols = nn(grouped, compress_w)
    compressed = by_core(comp_cols[:comp_part], cube.core_swap(comp_cols[comp_part:]), 1)
    token_f = tokens.astype(F32)
    keyed_rows = jnp.concatenate([compressed, memory.astype(F32), token_f], axis=0)
    attn_value, attn_pull = jax.vjp(rms_norm, keyed_rows, gain_attn_f)
    attn_normed = attn_value.astype(BF16)
    all_rows = jnp.concatenate([attn_normed, cube.core_swap(attn_normed)], axis=0)
    tok_at = comp_part + mem_part
    token_rows = jnp.concatenate([all_rows[tok_at:rows], all_rows[rows + tok_at :]], axis=0)
    query_rows = nn(token_rows, query_w, BF16)
    keyval = nn(all_rows, keyval_w, BF16)
    mixed, lse = attend(info, query_rows, keyval, parts, heads)

    def summed_share(full, other_side):
        away = cube.core_swap(nt(full[tok_part:], other_side, BF16))
        return nt(full[:tok_part], other_side) + away.astype(F32)

    attn_branch = summed_share(mixed, output_t)
    after_attn = token_f + attn_branch
    ffn_value, ffn_pull = jax.vjp(rms_norm, after_attn, gain_ffn_f)
    ffn_own = ffn_value.astype(BF16)
    ffn_rows = jnp.concatenate([ffn_own, cube.core_swap(ffn_own)], axis=0)
    inner_hidden = nn(ffn_rows, inner_w)
    active_f, gelu_pull = jax.vjp(gelu_tanh, inner_hidden)
    active = active_f.astype(BF16)
    ffn_branch = summed_share(active, outer_t)
    summed = after_attn + ffn_branch
    layer_output = summed.astype(BF16)
    square_sums = jnp.stack(
        [
            jnp.sum(attn_branch * attn_branch),
            jnp.sum(ffn_branch * ffn_branch),
            jnp.sum(summed * summed),
        ]
    )
    branch_rms = jnp.sqrt((square_sums + cube.core_swap(square_sums)) / (L * D))[None]

    def split(partial):
        return partial.reshape(n, partial.shape[0] // n, partial.shape[1])

    out_grads = jnp.concatenate([cotangent, cube.core_swap(cotangent)], axis=0)
    grad_outer = cube.reduce(*picked([split(tn(out_grads, active, BF16))])).T
    d_active = nn(out_grads, outer_t)
    d_inner = gelu_pull(d_active)[0].astype(BF16)
    d_ffn_normed = summed_share(d_inner, inner_w)
    d_after, d_gain_ffn = ffn_pull(d_ffn_normed)
    grad_after = cotangent.astype(F32) + d_after
    grad_after_own = grad_after.astype(BF16)
    attn_grads = jnp.concatenate([grad_after_own, cube.core_swap(grad_after_own)], axis=0)
    out_inner = cube.reduce(
        *picked([split(tn(attn_grads, mixed, BF16)), split(tn(ffn_rows, d_inner, BF16))]),
    )
    grad_output, grad_inner = out_inner[:, :width].T, out_inner[:, width:]
    d_mixed = nn(attn_grads, output_t, BF16)
    back = info, query_rows, keyval, mixed, d_mixed, lse, parts
    carry = attend_back(*back, 0, heads // 2)
    d_queries, d_keyval = attend_back(*back, heads // 2, heads - heads // 2, carry)
    near_qkv, far_qkv = picked(
        [split(tn(token_rows, d_queries, BF16)), split(tn(all_rows, d_keyval, BF16))]
    )
    qkv = cube.reduce(near_qkv, far_qkv)
    d_queries, d_keyval = lax.optimization_barrier((d_queries, d_keyval, near_qkv, far_qkv))[:2]
    grad_query = qkv[:, :width]
    key_cols = [qkv[:, width + 2 * h * DH :][:, :DH] for h in range(heads)]
    value_cols = [qkv[:, width + (2 * h + 1) * DH :][:, :DH] for h in range(heads)]
    grad_key = jnp.concatenate(key_cols, axis=1)
    grad_value = jnp.concatenate(value_cols, axis=1)
    d_rows = nt(d_keyval, keyval_w)
    d_tok = nt(d_queries, query_w)
    d_own = jnp.concatenate([d_rows[:tok_at], d_rows[tok_at:rows] + d_tok[:tok_part]], axis=0)
    d_other = jnp.concatenate(
        [d_rows[rows : rows + tok_at], d_rows[rows + tok_at :] + d_tok[tok_part:]], axis=0
    ).astype(BF16)
    d_attn_normed = d_own + cube.core_swap(d_other).astype(F32)
    d_keyed, d_gain_attn = attn_pull(d_attn_normed)
    input_grad = (grad_after + d_keyed[tok_at:]).astype(BF16)
    d_comp = d_keyed[:comp_part].astype(BF16)
    d_send = jnp.where(core > 0, d_comp[:, :col_half], d_comp[:, col_half:])
    d_keep = jnp.where(core > 0, d_comp[:, col_half:], d_comp[:, :col_half])
    d_comp_cols = jnp.concatenate([d_keep, cube.core_swap(d_send)], axis=0)
    d_gains = jnp.stack([d_gain_attn, d_gain_ffn]).reshape(2, n, 2 * share)
    d_gains = jnp.transpose(d_gains, (1, 0, 2)).reshape(n, 1, 4 * share).astype(BF16)
    d_gains = jnp.pad(d_gains, ((0, 0), (0, 15), (0, col_half - 4 * share)))
    last = cube.reduce(*picked([split(nn(grouped_t, d_comp_cols, BF16))], d_gains))
    mine = w_compress.shape[0]
    away = jnp.where(core > 0, last[:mine], last[mine : 2 * mine])
    kept = jnp.where(core > 0, last[mine : 2 * mine], last[:mine])
    arrived = cube.core_swap(jnp.concatenate([away, last[2 * mine : 2 * mine + 8]], axis=0))
    grad_compress = by_core(kept, arrived[:mine], 1)
    gain_sum = (last[2 * mine] + arrived[mine])[: 4 * share].reshape(2, 2, share)
    gain_sum = jnp.where(core > 0, gain_sum[:, 1], gain_sum[:, 0])
    return (
        layer_output[None],
        input_grad[None],
        grad_query,
        grad_key,
        grad_value,
        grad_output,
        grad_compress,
        gain_sum[0],
        gain_sum[1],
        grad_inner,
        grad_outer,
        branch_rms,
    )


def solution(mesh):
    in_specs = (
        P("dp", "tensor", None),
        P("dp", "tensor", None),
        P("dp", "tensor", None),
        P("dp"),
        P("dp", None),
        P("dp", "tensor"),
        P("dp", "tensor"),
        P("dp", "tensor"),
        P("tensor", "dp"),
        P(("dp", "tensor"), None),
        P(("dp", "tensor")),
        P(("dp", "tensor")),
        P("dp", "tensor"),
        P("tensor", "dp"),
        P("dp", "tensor", None),
    )
    out_specs = (
        P("dp", "tensor", None),
        P("dp", "tensor", None),
        P("dp", "tensor"),
        P("dp", "tensor"),
        P("dp", "tensor"),
        P("tensor", "dp"),
        P(("dp", "tensor"), None),
        P(("dp", "tensor")),
        P(("dp", "tensor")),
        P("dp", "tensor"),
        P("tensor", "dp"),
        P("dp", None),
    )

    return jax.shard_map(
        per_device, mesh=mesh, in_specs=in_specs, out_specs=out_specs, check_vma=False
    )
```

```python
import jax
import jax.numpy as jnp
from jax import lax
from jax.experimental import pallas as pl
from jax.experimental.pallas import tpu as pltpu
from jax.sharding import PartitionSpec as P


D = 1024
DH = 128
MEM = 512
CMEM = 512
PIC = 256
L = 1024

epsilon = 1e-06
very_negative = -1e30


F32 = jnp.float32
BF16 = jnp.bfloat16
AXES = ("dp", "tensor")


def matmul(a, b, dims, out=F32):
    return lax.dot_general(a, b, (dims, ((), ())), preferred_element_type=F32).astype(out)


def nn(a, b, out=F32):
    return matmul(a, b, ((1,), (0,)), out)


def nt(a, b, out=F32):
    return matmul(a, b, ((1,), (1,)), out)


def tn(a, b, out=F32):
    return matmul(a, b, ((0,), (0,)), out)


class Cube:
    def __init__(self, n, cores):
        self.n, self.cores = n, cores
        self.far = n // 4
        self.low = [(1, 0) if c % 2 == 0 else (0, 1) for c in range(cores)]
        self.masks = [
            [
                (j % self.far) * 4
                + ((j // self.far) & 1) * (1 << first)
                + (j // (2 * self.far)) * (1 << second)
                for j in range(n)
            ]
            for first, second in self.low
        ]
        self.dp = lax.axis_index("dp")
        self.core = lax.axis_index("tensor")
        table = jnp.array(self.masks, jnp.int32)
        self.own = lax.dynamic_index_in_dim(table, self.core, 0, keepdims=False) ^ self.dp

    def send(self, value, flips):
        pairs = [
            (d * self.cores + c, (d ^ flips[c]) * self.cores + c)
            for d in range(self.n)
            for c in range(self.cores)
        ]
        return lax.ppermute(value, AXES, pairs)

    def far_send(self, value, m):
        return self.send(value, [4 * m] * self.cores)

    def low_swap(self, value, which):
        return self.send(value, [1 << pair[which] for pair in self.low])

    def core_swap(self, value):
        return lax.ppermute(value, "tensor", [(0, 1), (1, 0)])

    def reduce(self, low, high):
        arrived = self.low_swap(high, 1)
        half = low.shape[0] // 2

        def added(part, other, run):
            return part[run].astype(F32) + other[run].astype(F32)

        far = slice(half, None)
        near = added(low, arrived, slice(0, half)).astype(BF16)
        far_sum = added(low, arrived, far).astype(BF16)
        arrived = self.low_swap(far_sum, 0)
        total = near[0].astype(F32) + arrived[0].astype(F32)
        sent = [
            self.far_send(added(near, arrived, slice(m, m + 1)).astype(BF16), m)
            for m in range(1, self.far)
        ]
        for block in sent:
            total = total + block[0].astype(F32)
        return total


ANY = pl.BlockSpec(memory_space=pl.ANY)
SMEM = pl.BlockSpec(memory_space=pltpu.SMEM)
VMEM = pl.BlockSpec(memory_space=pltpu.VMEM)


def run_copies(copies):
    for copy in copies:
        copy.start()
    for copy in copies:
        copy.wait()


def place(parts, where, pieces, outs):
    rows = parts[0].shape[1]
    count = where.shape[0]

    def body(where_ref, *refs):
        ins, out_refs, sem = refs[: len(parts)], refs[len(parts) : -1], refs[-1]
        copies, j = [], 0
        for source in ins:
            for b in range(source.shape[0]):
                at = 0
                for i, (width, out, row) in enumerate(pieces):
                    copies.append(
                        pltpu.make_async_copy(
                            source.at[b, :, pl.ds(at, width)],
                            out_refs[out].at[where_ref[j], pl.ds(row, rows)],
                            sem.at[j * len(pieces) + i],
                        )
                    )
                    at += width
                j += 1
        run_copies(copies)

    filled = pl.pallas_call(
        body,
        out_shape=[jax.ShapeDtypeStruct((count, r, w), parts[0].dtype) for r, w in outs],
        in_specs=[SMEM] + [ANY] * len(parts),
        out_specs=[VMEM] * len(outs),
        scratch_shapes=[pltpu.SemaphoreType.DMA((count * len(pieces),))],
        name="place",
    )(where, *parts)
    return [o.reshape(count * r, w) for o, (r, w) in zip(filled, outs)]


def pick(blocks, where, below=None):
    count = where.shape[0]
    rows = blocks[0].shape[1]
    width = sum(b.shape[2] for b in blocks)
    half = count // 2
    ins = list(blocks) + ([] if below is None else [below])
    total = rows + (0 if below is None else below.shape[1])

    def body(where_ref, *refs):
        sources, (low, high, sem) = refs[: len(ins)], refs[len(ins) :]
        copies = []
        for j in range(count):
            at = 0
            out = (low if j < half else high).at[j % half]
            for i, source in enumerate(sources):
                if i < len(blocks):
                    target = out.at[pl.ds(0, rows), pl.ds(at, source.shape[2])]
                    at += source.shape[2]
                else:
                    target = out.at[pl.ds(rows, source.shape[1])]
                copies.append(
                    pltpu.make_async_copy(
                        source.at[where_ref[j]], target, sem.at[j * len(ins) + i]
                    )
                )
        run_copies(copies)

    return pl.pallas_call(
        body,
        out_shape=[jax.ShapeDtypeStruct((half, total, width), BF16)] * 2,
        in_specs=[SMEM] + [ANY] * len(ins),
        out_specs=[VMEM] * 2,
        scratch_shapes=[pltpu.SemaphoreType.DMA((count * len(ins),))],
        name="pick",
    )(where, *ins)


def rms_norm(matrix_rows, gain_vec):
    return (
        matrix_rows
        * lax.rsqrt(jnp.mean(matrix_rows * matrix_rows, axis=-1, keepdims=True) + epsilon)
        * gain_vec
    )


def gelu_tanh(inner_in):
    return jax.nn.gelu(inner_in, approximate=True)


LOG2E = 1.4426950408889634


def key_runs(core, half, kind, part_rows, comp_part, mem_part):
    base = jnp.bitwise_xor(core, half) * part_rows
    offset = {"comp": 0, "mem": comp_part, "tok": comp_part + mem_part}[kind]
    return pl.multiple_of(base + offset, 128)


def attention_chunks(info, q_half, shapes):
    comp_part, mem_part, tok_part = shapes
    part_rows = comp_part + mem_part + tok_part
    core, span, mem_len, comp_len = info[0], info[1], info[2], info[3]

    def start(kind, half):
        return key_runs(core, half, kind, part_rows, comp_part, mem_part)

    def tail(first, total, length):
        def masker(shape):
            row = lax.broadcasted_iota(jnp.int32, shape, 0) + first
            return row >= total - length

        return masker

    def causal(half):
        def masker(shape):
            key = lax.broadcasted_iota(jnp.int32, shape, 0) + half * tok_part
            query = lax.broadcasted_iota(jnp.int32, shape, 1) + q_half * tok_part
            key_in = (key >= span) & (key < span + PIC)
            query_in = (query >= span) & (query < span + PIC)
            return (key <= query) | (key_in & query_in)

        return masker

    chunks = []
    for half in (0, 1):
        chunks.append((start("comp", half), comp_part, tail(half * comp_part, CMEM, comp_len), None))
    for half in (0, 1):
        chunks.append((start("mem", half), mem_part, tail(half * mem_part, MEM, mem_len), None))
    crosses = (span < tok_part) & (span + PIC > tok_part)
    chunks.append((start("tok", 0), tok_part, causal(0), None))
    chunks.append((start("tok", 1), tok_part, causal(1), (q_half == 1) | crosses))
    return chunks


def attend(info, query_rows, keyval, shapes, heads):
    rows = keyval.shape[0]
    q_part = query_rows.shape[0] // 2
    factor = DH ** (-0.5) * LOG2E

    def body(info_ref, q_ref, kv_ref, o_ref, lse_ref, vt_ref, s_ref, m_ref, l_ref, acc_ref):
        q_half = pl.program_id(1)

        @pl.when(q_half == 0)
        def _():
            vt_ref[...] = kv_ref[:, DH:].T

        q = q_ref[...]
        chunks = attention_chunks(info_ref, q_half, shapes)
        always = [c for c in chunks if c[3] is None]
        (first1, count1, masker1, needed1) = next(c for c in chunks if c[3] is not None)
        spots = [sum(c[1] for c in always[:i]) for i in range(len(always) + 1)]

        def fold(values):
            return values.reshape(-1, 8, values.shape[1])

        def scores(first, count, masker, spot):
            s = nt(kv_ref[pl.ds(first, count), :DH], q)
            s = jnp.where(masker(s.shape), s, very_negative)
            s_ref[spot : spot + count, :] = s
            return jnp.max(fold(s), axis=0)

        def weigh(first, count, spot, top):
            p = jnp.exp2((s_ref[spot : spot + count, :] - top) * factor)
            return jnp.sum(fold(p), axis=0), nn(vt_ref[:, pl.ds(first, count)], p.astype(BF16))

        peak = None
        for (first, count, masker, _), spot in zip(always, spots):
            here = scores(first, count, masker, spot)
            peak = here if peak is None else jnp.maximum(peak, here)
        m_ref[...] = peak

        @pl.when(needed1)
        def _():
            m_ref[...] = jnp.maximum(m_ref[...], scores(first1, count1, masker1, spots[-1]))

        top = jnp.max(m_ref[...], axis=0, keepdims=True)
        total, acc = None, None
        for (first, count, _, _), spot in zip(always, spots):
            part, product = weigh(first, count, spot, top)
            total = part if total is None else total + part
            acc = product if acc is None else acc + product
        l_ref[...] = total
        acc_ref[...] = acc

        @pl.when(needed1)
        def _():
            part, product = weigh(first1, count1, spots[-1], top)
            l_ref[...] += part
            acc_ref[...] += product

        total = jnp.sum(l_ref[...], axis=0, keepdims=True)
        o_ref[...] = (acc_ref[...] / total).T.astype(BF16)
        lse_ref[...] = (top * factor + jnp.log2(total))[None]

    def q_map(h, a, info_ref):
        return (jnp.bitwise_xor(a, info_ref[0]), h)

    return pl.pallas_call(
        body,
        out_shape=(
            jax.ShapeDtypeStruct(query_rows.shape, BF16),
            jax.ShapeDtypeStruct((heads * 2, 1, q_part), F32),
        ),
        grid_spec=pltpu.PrefetchScalarGridSpec(
            num_scalar_prefetch=1,
            grid=(heads, 2),
            in_specs=[
                pl.BlockSpec((q_part, DH), q_map),
                pl.BlockSpec((rows, 2 * DH), lambda h, a, i: (0, h)),
            ],
            out_specs=[
                pl.BlockSpec((q_part, DH), q_map),
                pl.BlockSpec((1, 1, q_part), lambda h, a, i: (h * 2 + a, 0, 0)),
            ],
            scratch_shapes=[
                pltpu.VMEM((DH, rows), BF16),
                pltpu.VMEM((rows, q_part), F32),
                pltpu.VMEM((8, q_part), F32),
                pltpu.VMEM((8, q_part), F32),
                pltpu.VMEM((DH, q_part), F32),
            ],
        ),
        name="attend",
    )(info, query_rows, keyval)


def attend_back(info, query_rows, keyval, mixed, d_mixed, lse, shapes, skip, heads, carry=None):
    rows = keyval.shape[0]
    q_part = query_rows.shape[0] // 2
    scale = DH ** (-0.5)
    factor = scale * LOG2E

    def body(info_ref, q_ref, kv_ref, o_ref, g_ref, lse_ref, *refs):
        dq_ref, dkv_ref, kt_ref, dk_acc, dv_acc, dq_acc = refs[-6:]
        q_half = pl.program_id(1)

        @pl.when(q_half == 0)
        def _():
            kt_ref[...] = kv_ref[:, :DH].T
            dk_acc[...] = jnp.zeros_like(dk_acc)
            dv_acc[...] = jnp.zeros_like(dv_acc)

        dq_acc[...] = jnp.zeros_like(dq_acc)
        q, g = q_ref[...], g_ref[...]
        lse_row = lse_ref[0]
        delta = jnp.sum((g.astype(F32) * o_ref[...].astype(F32)).T, axis=0, keepdims=True)
        for first, count, masker, needed in attention_chunks(info_ref, q_half, shapes):

            def step(first=first, count=count, masker=masker):
                run = pl.ds(first, count)
                p = jnp.exp2(nt(kv_ref[run, :DH], q) * factor - lse_row)
                if masker is not None:
                    p = jnp.where(masker(p.shape), p, 0.0)
                d_p = nt(kv_ref[run, DH:], g)
                d_s = (p * (d_p - delta)).astype(BF16)
                dv_acc[run, :] += nn(p.astype(BF16), g)
                dk_acc[run, :] += nn(d_s, q)
                dq_acc[...] += nn(kt_ref[:, run], d_s)

            if needed is None:
                step()
            else:
                pl.when(needed)(step)
        dq_ref[...] = (dq_acc[...] * scale).T.astype(BF16)

        @pl.when(q_half == 1)
        def _():
            dkv_ref[:, :DH] = (dk_acc[...] * scale).astype(BF16)
            dkv_ref[:, DH:] = dv_acc[...].astype(BF16)

    def q_map(h, a, info_ref):
        return (jnp.bitwise_xor(a, info_ref[0]), h + skip)

    q_spec = pl.BlockSpec((q_part, DH), q_map)
    kv_spec = pl.BlockSpec((rows, 2 * DH), lambda h, a, i: (0, h + skip))
    lse_spec = pl.BlockSpec((1, 1, q_part), lambda h, a, i: ((h + skip) * 2 + a, 0, 0))
    carried = [] if carry is None else list(carry)
    return pl.pallas_call(
        body,
        out_shape=(
            jax.ShapeDtypeStruct(query_rows.shape, BF16),
            jax.ShapeDtypeStruct(keyval.shape, BF16),
        ),
        grid_spec=pltpu.PrefetchScalarGridSpec(
            num_scalar_prefetch=1,
            grid=(heads, 2),
            in_specs=[q_spec, kv_spec, q_spec, q_spec, lse_spec] + [ANY] * len(carried),
            out_specs=[q_spec, kv_spec],
            scratch_shapes=[
                pltpu.VMEM((DH, rows), BF16),
                pltpu.VMEM((rows, DH), F32),
                pltpu.VMEM((rows, DH), F32),
                pltpu.VMEM((DH, q_part), F32),
            ],
        ),
        input_output_aliases={6 + i: i for i in range(len(carried))},
        name="attend_back",
    )(info, query_rows, keyval, mixed, d_mixed, lse, *carried)


def per_device(
    layer_input,
    memory,
    evicted,
    picture_start,
    memory_lengths,
    w_query,
    w_key,
    w_value,
    w_output,
    w_compress,
    gain_attn,
    gain_ffn,
    w_inner,
    w_outer,
    cotangent,
):
    cube = Cube(lax.axis_size("dp"), lax.axis_size("tensor"))
    n, core = cube.n, cube.core
    tokens, memory, evicted, cotangent = layer_input[0], memory[0], evicted[0], cotangent[0]
    tok_part, mem_part, comp_part = tokens.shape[0], memory.shape[0], evicted.shape[0] // 3
    parts = (comp_part, mem_part, tok_part)
    width = w_query.shape[1]
    heads = width // DH
    rows = comp_part + mem_part + tok_part
    inner_width = w_inner.shape[1]
    share = gain_attn.shape[0]
    shard_rows = w_query.shape[0]

    def by_core(own, other, axis):
        flip = core > 0
        return jnp.concatenate(
            [jnp.where(flip, other, own), jnp.where(flip, own, other)], axis=axis
        )

    def gathered(shard, pieces, outs):
        held = [shard[None]] + [cube.far_send(shard[None], m) for m in range(1, cube.far)]
        held = jnp.concatenate(held, axis=0)
        near = cube.low_swap(held, 0)
        own_far = cube.low_swap(held, 1)
        far = cube.low_swap(near, 1)
        return place([held, near, own_far, far], cube.own, pieces, outs)

    def picked(blocks, below=None):
        return pick(blocks, cube.own, below)

    col_half = D // 2
    send_cols = jnp.where(core > 0, w_compress[:, :col_half], w_compress[:, col_half:])
    keep_cols = jnp.where(core > 0, w_compress[:, col_half:], w_compress[:, :col_half])
    compress_cols = by_core(keep_cols, cube.core_swap(send_cols), 0)
    gains_own = jnp.stack([gain_attn, gain_ffn])
    gain_pair = by_core(gains_own[None], cube.core_swap(gains_own)[None], 0)
    gain_row = jnp.pad(gain_pair.reshape(1, -1), ((0, shard_rows - 1), (0, 128 - 4 * share)))
    columns = [w_query]
    for h in range(heads):
        head = slice(h * DH, (h + 1) * DH)
        columns += [w_key[:, head], w_value[:, head]]
    columns += [gain_row]
    folds = compress_cols.shape[0] // shard_rows
    columns += [compress_cols[i * shard_rows : (i + 1) * shard_rows] for i in range(folds)]
    query_w, keyval_w, gain_rows, compress_w = gathered(
        jnp.concatenate(columns, axis=1),
        [(width, 0, 0), (2 * width, 1, 0), (128, 2, 0)]
        + [(col_half, 3, i * shard_rows) for i in range(folds)],
        [
            (shard_rows, width),
            (shard_rows, 2 * width),
            (shard_rows, 128),
            (folds * shard_rows, col_half),
        ],
    )
    output_t, inner_w = gathered(
        jnp.concatenate([w_output.T, w_inner], axis=1),
        [(width, 0, 0), (inner_width, 1, 0)],
        [(shard_rows, width), (shard_rows, inner_width)],
    )
    (outer_t,) = gathered(w_outer.T, [(inner_width, 0, 0)], [(shard_rows, inner_width)])
    gains = gain_rows.reshape(n, shard_rows, 128)[:, 0, : 4 * share].reshape(n, 2, 2, share)
    gains = jnp.transpose(gains, (2, 0, 1, 3)).reshape(2, D).astype(F32)
    gain_attn_f, gain_ffn_f = gains[0], gains[1]

    info = jnp.concatenate([core[None], picture_start, memory_lengths[0]]).astype(jnp.int32)
    grouped_own = evicted.reshape(comp_part, 3 * D)
    grouped = jnp.concatenate([grouped_own, cube.core_swap(grouped_own)], axis=0)
    grouped_t = lax.optimization_barrier(grouped.T)
    comp_cols = nn(grouped, compress_w)
    compressed = by_core(comp_cols[:comp_part], cube.core_swap(comp_cols[comp_part:]), 1)
    token_f = tokens.astype(F32)
    keyed_rows = jnp.concatenate([compressed, memory.astype(F32), token_f], axis=0)
    attn_value, attn_pull = jax.vjp(rms_norm, keyed_rows, gain_attn_f)
    attn_normed = attn_value.astype(BF16)
    all_rows = jnp.concatenate([attn_normed, cube.core_swap(attn_normed)], axis=0)
    tok_at = comp_part + mem_part
    token_rows = jnp.concatenate([all_rows[tok_at:rows], all_rows[rows + tok_at :]], axis=0)
    query_rows = nn(token_rows, query_w, BF16)
    keyval = nn(all_rows, keyval_w, BF16)
    mixed, lse = attend(info, query_rows, keyval, parts, heads)

    def summed_share(full, other_side):
        away = cube.core_swap(nt(full[tok_part:], other_side, BF16))
        return nt(full[:tok_part], other_side) + away.astype(F32)

    attn_branch = summed_share(mixed, output_t)
    after_attn = token_f + attn_branch
    ffn_value, ffn_pull = jax.vjp(rms_norm, after_attn, gain_ffn_f)
    ffn_own = ffn_value.astype(BF16)
    ffn_rows = jnp.concatenate([ffn_own, cube.core_swap(ffn_own)], axis=0)
    inner_hidden = nn(ffn_rows, inner_w)
    active_f, gelu_pull = jax.vjp(gelu_tanh, inner_hidden)
    active = active_f.astype(BF16)
    ffn_branch = summed_share(active, outer_t)
    summed = after_attn + ffn_branch
    layer_output = summed.astype(BF16)
    square_sums = jnp.stack(
        [
            jnp.sum(attn_branch * attn_branch),
            jnp.sum(ffn_branch * ffn_branch),
            jnp.sum(summed * summed),
        ]
    )
    branch_rms = jnp.sqrt((square_sums + cube.core_swap(square_sums)) / (L * D))[None]

    def split(partial):
        return partial.reshape(n, partial.shape[0] // n, partial.shape[1])

    out_grads = jnp.concatenate([cotangent, cube.core_swap(cotangent)], axis=0)
    grad_outer = cube.reduce(*picked([split(tn(out_grads, active, BF16))])).T
    d_active = nn(out_grads, outer_t)
    d_inner = gelu_pull(d_active)[0].astype(BF16)
    d_ffn_normed = summed_share(d_inner, inner_w)
    d_after, d_gain_ffn = ffn_pull(d_ffn_normed)
    grad_after = cotangent.astype(F32) + d_after
    grad_after_own = grad_after.astype(BF16)
    attn_grads = jnp.concatenate([grad_after_own, cube.core_swap(grad_after_own)], axis=0)
    out_inner = cube.reduce(
        *picked([split(tn(attn_grads, mixed, BF16)), split(tn(ffn_rows, d_inner, BF16))]),
    )
    grad_output, grad_inner = out_inner[:, :width].T, out_inner[:, width:]
    d_mixed = nn(attn_grads, output_t, BF16)
    back = info, query_rows, keyval, mixed, d_mixed, lse, parts
    carry = attend_back(*back, 0, heads // 2)
    d_queries, d_keyval = attend_back(*back, heads // 2, heads - heads // 2, carry)
    near_qkv, far_qkv = picked(
        [split(tn(token_rows, d_queries, BF16)), split(tn(all_rows, d_keyval, BF16))]
    )
    qkv = cube.reduce(near_qkv, far_qkv)
    d_queries, d_keyval = lax.optimization_barrier((d_queries, d_keyval, near_qkv, far_qkv))[:2]
    grad_query = qkv[:, :width]
    key_cols = [qkv[:, width + 2 * h * DH :][:, :DH] for h in range(heads)]
    value_cols = [qkv[:, width + (2 * h + 1) * DH :][:, :DH] for h in range(heads)]
    grad_key = jnp.concatenate(key_cols, axis=1)
    grad_value = jnp.concatenate(value_cols, axis=1)
    d_rows = nt(d_keyval, keyval_w)
    d_tok = nt(d_queries, query_w)
    d_own = jnp.concatenate([d_rows[:tok_at], d_rows[tok_at:rows] + d_tok[:tok_part]], axis=0)
    d_other = jnp.concatenate(
        [d_rows[rows : rows + tok_at], d_rows[rows + tok_at :] + d_tok[tok_part:]], axis=0
    ).astype(BF16)
    d_attn_normed = d_own + cube.core_swap(d_other).astype(F32)
    d_keyed, d_gain_attn = attn_pull(d_attn_normed)
    input_grad = (grad_after + d_keyed[tok_at:]).astype(BF16)
    d_comp = d_keyed[:comp_part].astype(BF16)
    d_send = jnp.where(core > 0, d_comp[:, :col_half], d_comp[:, col_half:])
    d_keep = jnp.where(core > 0, d_comp[:, col_half:], d_comp[:, :col_half])
    d_comp_cols = jnp.concatenate([d_keep, cube.core_swap(d_send)], axis=0)
    d_gains = jnp.stack([d_gain_attn, d_gain_ffn]).reshape(2, n, 2 * share)
    d_gains = jnp.transpose(d_gains, (1, 0, 2)).reshape(n, 1, 4 * share).astype(BF16)
    d_gains = jnp.pad(d_gains, ((0, 0), (0, 15), (0, col_half - 4 * share)))
    last = cube.reduce(*picked([split(nn(grouped_t, d_comp_cols, BF16))], d_gains))
    mine = w_compress.shape[0]
    away = jnp.where(core > 0, last[:mine], last[mine : 2 * mine])
    kept = jnp.where(core > 0, last[mine : 2 * mine], last[:mine])
    arrived = cube.core_swap(jnp.concatenate([away, last[2 * mine : 2 * mine + 8]], axis=0))
    grad_compress = by_core(kept, arrived[:mine], 1)
    gain_sum = (last[2 * mine] + arrived[mine])[: 4 * share].reshape(2, 2, share)
    gain_sum = jnp.where(core > 0, gain_sum[:, 1], gain_sum[:, 0])
    return (
        layer_output[None],
        input_grad[None],
        grad_query,
        grad_key,
        grad_value,
        grad_output,
        grad_compress,
        gain_sum[0],
        gain_sum[1],
        grad_inner,
        grad_outer,
        branch_rms,
    )


def solution(mesh):
    in_specs = (
        P("dp", "tensor", None),
        P("dp", "tensor", None),
        P("dp", "tensor", None),
        P("dp"),
        P("dp", None),
        P("dp", "tensor"),
        P("dp", "tensor"),
        P("dp", "tensor"),
        P("tensor", "dp"),
        P(("dp", "tensor"), None),
        P(("dp", "tensor")),
        P(("dp", "tensor")),
        P("dp", "tensor"),
        P("tensor", "dp"),
        P("dp", "tensor", None),
    )
    out_specs = (
        P("dp", "tensor", None),
        P("dp", "tensor", None),
        P("dp", "tensor"),
        P("dp", "tensor"),
        P("dp", "tensor"),
        P("tensor", "dp"),
        P(("dp", "tensor"), None),
        P(("dp", "tensor")),
        P(("dp", "tensor")),
        P("dp", "tensor"),
        P("tensor", "dp"),
        P("dp", None),
    )

    return jax.shard_map(
        per_device, mesh=mesh, in_specs=in_specs, out_specs=out_specs, check_vma=False
    )
```
